32 devices in a mesh: seq: 8 (over y, x, core), tp: 4 (over z).
Axes of the slice: x: 2, y: 2, z: 4, core: 2. Of those that a mesh axis runs over, the one named last changes fastest.
Arguments:
- hidden: bfloat16 [5120, 2048], P('seq', 'tp'), may hold values from -12 to 12
- w_qkv: bfloat16 [3, 2048, 2048], P(None, None, 'tp')
- w_out: bfloat16 [2048, 2048], P('tp'), may hold values from -0.125 to 0.125
- seg_ids: int32 [5120], P('seq'), may hold values from 0 to 16, as said below
- positions: int32 [5120], P('seq'), may hold values from 0 to 4095, as said below
- page_table: int32 [320], P('seq'), may hold values from 0 to 319, as said below
Outputs:
- delta: bfloat16 [5120, 2048], P('seq', 'tp')
- k_cache: bfloat16 [320, 16, 2048], P('seq', None, 'tp')
- v_cache: bfloat16 [320, 16, 2048], P('seq', None, 'tp')
The draws below stay inside these ranges and needn't reach their ends.
Inputs may be any that keep to these rules, and one draw needn't show every extreme that they name: `seg_ids`: tokens 0 to 4095 form prompt 0; the remaining tokens form prompts 1 to 16 in order, each of 16 to 112 tokens. `positions`: positions rise by one from token to token inside a prompt; prompt 0 starts at 0, every other prompt at a value below 256. `page_table`: every page appears once; page p lives on index p // 40 of seq; the pages of one index of seq go to at most 5 pages of any one owner, and exactly 5 to some owner.
All inputs are finite; a program needn't handle non-finite values.
Results may differ from the reference program's by a relative error of at most 0.0076.
Values may be sent and summed in bfloat16 or wider, within the bound.
A program may use at most 320 MiB of HBM per device.

```python
import math
import jax
import jax.numpy as jnp
from jax import lax

D = 2048
HEADS = 16
HEAD_DIM = 128
PAGE = 16
TOK_DEV = 640
TOKENS = 5120
LONG = 4096
SHORTS = 16
PAGES = 320
BLOCKS_DEV = 40


def short_layout(key):
    inner_key = jax.random.fold_in(key, 5)
    jitter = jax.random.randint(inner_key, (SHORTS,), -24, 25)
    cut_index = jnp.arange(SHORTS, dtype=jnp.int32)
    starts = LONG + 64 * cut_index + jnp.where(cut_index > 0, jitter, 0)
    token_index = jnp.arange(TOKENS, dtype=jnp.int32)
    segment = jnp.sum((token_index[:, None] >= starts[None, :]).astype(jnp.int32), axis=1)
    offsets = jax.random.randint(jax.random.fold_in(key, 6), (SHORTS,), 0, 256)
    start_table = jnp.concatenate([jnp.zeros((1,), jnp.int32), starts.astype(jnp.int32)])
    offset_table = jnp.concatenate([jnp.zeros((1,), jnp.int32), offsets.astype(jnp.int32)])
    position = token_index - start_table[segment] + offset_table[segment]
    return (segment.astype(jnp.int32), position.astype(jnp.int32))


def draw_seg_ids(key, part):
    return short_layout(key)[0]


def draw_positions(key, part):
    return short_layout(key)[1]


def draw_page_table(key, part):
    devices = PAGES // BLOCKS_DEV
    rotation = jax.random.randint(jax.random.fold_in(key, 21), (), 0, devices)
    order_keys = jax.random.split(jax.random.fold_in(key, 22), devices)
    order = jax.vmap(lambda one_key: jax.random.permutation(one_key, BLOCKS_DEV))(order_keys).astype(jnp.int32)
    source = jnp.arange(devices, dtype=jnp.int32)[:, None]
    owner = (source + (order + rotation) % devices) % devices
    occurrence = order // devices
    quotient = BLOCKS_DEV // devices
    remainder = BLOCKS_DEV % devices
    owner_index = jnp.arange(devices, dtype=jnp.int32)[None, :]
    counts = quotient + ((owner_index - source - rotation) % devices < remainder).astype(jnp.int32)
    earlier = jnp.cumsum(counts, axis=0) - counts
    source_full = jnp.broadcast_to(source, owner.shape)
    slot = earlier[source_full, owner] + occurrence
    shuffle_keys = jax.random.split(jax.random.fold_in(key, 23), devices)
    shuffle = jax.vmap(lambda one_key: jax.random.permutation(one_key, BLOCKS_DEV))(shuffle_keys).astype(jnp.int32)
    page = owner * BLOCKS_DEV + shuffle[owner, slot]
    return page.reshape(PAGES).astype(jnp.int32)


def draw_hidden(key, part):
    column_scale = jnp.exp(jax.random.uniform(jax.random.fold_in(key, 31), (D,), jnp.float32, 0.0, math.log(10.0)))
    regions = jax.random.normal(jax.random.fold_in(key, 32), (TOKENS // 128 + 1, D), jnp.float32)
    token_index = jnp.arange(TOKENS)
    region_part = regions[token_index // 128]
    noise = jax.random.normal(jax.random.fold_in(key, 33), (TOKENS, D), jnp.float32)
    offset = 0.5 * jax.random.normal(jax.random.fold_in(key, 34), (TOKENS, 1), jnp.float32)
    base = 0.5 * noise * column_scale[None, :] + region_part + offset
    return jnp.clip(base, -12.0, 12.0).astype(jnp.bfloat16)


def draw_w_qkv(key, part):
    spread = D ** (-0.5)
    base = jnp.clip(jax.random.normal(jax.random.fold_in(key, 11), (3, D, D), jnp.float32), -4.5, 4.5) * spread
    return base.astype(jnp.bfloat16)


def block_scale(key, extent, pieces, low, largest):
    def one(dim, shards_of):
        steps = jax.random.uniform(jax.random.fold_in(jax.random.fold_in(key, 6), dim), (shards_of,), jnp.float32, low / len(pieces), largest / len(pieces))
        return jnp.repeat(jnp.exp(steps), extent[dim] // shards_of).reshape((-1,) + (1,) * (len(extent) - dim - 1))

    loudness = one(*pieces[0])
    for cut in pieces[1:]:
        loudness = loudness * one(*cut)
    return loudness


def normal_values(stream_key, extent, width, most, cuts=(), kind=jnp.bfloat16):
    loudness = block_scale(stream_key, extent, cuts, -0.22, 0.18) if cuts else 1.0
    entries = jax.random.normal(stream_key, extent, jnp.float32) * width * loudness
    return jnp.minimum(jnp.maximum(entries, -most), most).astype(kind)


def setup_inputs(seed: int = 0) -> dict:
    seeds = jax.random.split(jax.random.key(seed), 7)
    return {
        "hidden": draw_hidden(jax.random.fold_in(seeds[6], 71), 0),
        "w_qkv": draw_w_qkv(jax.random.fold_in(seeds[6], 71), 0),
        "w_out": normal_values(seeds[2], (D, D), D ** -0.5, 0.125, ((0, 4),)),
        "seg_ids": draw_seg_ids(jax.random.fold_in(seeds[6], 71), 0),
        "positions": draw_positions(jax.random.fold_in(seeds[6], 71), 0),
        "page_table": draw_page_table(jax.random.fold_in(seeds[6], 71), 0),
    }


ROPE_BASE = 10000.0
EPSILON = 1e-05
NEG_LARGE = -1e+30

def rope_tables(position_ids, head_width):
    half_width = head_width // 2
    frequency = ROPE_BASE ** (-jnp.arange(half_width).astype(jnp.float32) * 2.0 / head_width)
    angle = position_ids.astype(jnp.float32)[:, None] * frequency[None, :]
    return (jnp.cos(angle), jnp.sin(angle))

def rotate(vectors, cosine, sine_part):
    half_width = vectors.shape[-1] // 2
    first_half = vectors[..., :half_width]
    second_half = vectors[..., half_width:]
    cos_rows = cosine[:, None, :]
    sin_rows = sine_part[:, None, :]
    return jnp.concatenate([first_half * cos_rows - second_half * sin_rows, second_half * cos_rows + first_half * sin_rows], axis=-1)

def reference(hidden, w_qkv, w_out, seg_ids, positions, page_table):
    tok_rows = hidden.astype(jnp.float32)
    row_mean = lax.optimization_barrier(jnp.mean(tok_rows, axis=1, keepdims=True))
    centred = tok_rows - row_mean
    row_var = lax.optimization_barrier(jnp.mean(centred * centred, axis=1, keepdims=True))
    normed = (centred * lax.rsqrt(row_var + EPSILON)).astype(jnp.bfloat16)
    projected = [jnp.dot(normed, w_qkv[index], preferred_element_type=jnp.float32) for index in range(3)]
    cosine, sine_part = rope_tables(positions, HEAD_DIM)
    queries = rotate(projected[0].reshape(TOKENS, HEADS, HEAD_DIM), cosine, sine_part).astype(jnp.bfloat16)
    key_heads = rotate(projected[1].reshape(TOKENS, HEADS, HEAD_DIM), cosine, sine_part).astype(jnp.bfloat16)
    values = projected[2].astype(jnp.bfloat16)
    key_wide = key_heads.astype(jnp.float32)
    value_wide = values.reshape(TOKENS, HEADS, HEAD_DIM).astype(jnp.float32)
    score_scale = HEAD_DIM ** (-0.5)
    block_rows = 256 if TOKENS % 256 == 0 else TOK_DEV
    block_count = TOKENS // block_rows

    def attend_block(operands):
        query_block, seg_block, pos_block = operands
        scores = jnp.einsum('qhe,khe->qhk', query_block.astype(jnp.float32), key_wide) * score_scale
        visible = (seg_ids[None, :] == seg_block[:, None]) & (positions[None, :] <= pos_block[:, None])
        scores = jnp.where(visible[:, None, :], scores, NEG_LARGE)
        row_max = lax.optimization_barrier(jnp.max(scores, axis=2, keepdims=True))
        weights = jnp.where(visible[:, None, :], jnp.exp(scores - row_max), 0.0)
        weight_sum = lax.optimization_barrier(jnp.sum(weights, axis=2))
        probs = lax.optimization_barrier(weights.astype(jnp.bfloat16)).astype(jnp.float32)
        mixed = jnp.einsum('qhk,khe->qhe', probs, value_wide)
        return (mixed / weight_sum[:, :, None]).astype(jnp.bfloat16)
    attended = lax.map(attend_block, (queries.reshape(block_count, block_rows, HEADS, HEAD_DIM), seg_ids.reshape(block_count, block_rows), positions.reshape(block_count, block_rows)))
    attended = attended.reshape(TOKENS, D)
    delta = jnp.dot(attended, w_out, preferred_element_type=jnp.float32).astype(jnp.bfloat16)
    key_pages = key_heads.reshape(PAGES, PAGE, D)
    value_pages = values.reshape(PAGES, PAGE, D)
    k_cache = jnp.zeros((PAGES, PAGE, D), jnp.bfloat16).at[page_table].set(key_pages)
    v_cache = jnp.zeros((PAGES, PAGE, D), jnp.bfloat16).at[page_table].set(value_pages)
    return (delta, k_cache, v_cache)
```

```python
import jax
import jax.numpy as jnp
from jax import lax
from jax.sharding import PartitionSpec as P

HEAD_DIM = 128
PAGE = 16


ROPE_BASE = 10000.0
EPSILON = 1e-05
NEG_LARGE = -1e30


def rope_tables(position_ids, head_width):
    half_width = head_width // 2
    frequency = ROPE_BASE ** (-jnp.arange(half_width).astype(jnp.float32) * 2.0 / head_width)
    angle = position_ids.astype(jnp.float32)[:, None] * frequency[None, :]
    return (jnp.cos(angle), jnp.sin(angle))


def rotate(vectors, cosine, sine_part):
    half_width = vectors.shape[-1] // 2
    first_half = vectors[..., :half_width]
    second_half = vectors[..., half_width:]
    cos_rows = cosine[:, None, :]
    sin_rows = sine_part[:, None, :]
    return jnp.concatenate(
        [
            first_half * cos_rows - second_half * sin_rows,
            second_half * cos_rows + first_half * sin_rows,
        ],
        axis=-1,
    )


def fresh_state(query_heads):
    head_count, query_count, head_width = query_heads.shape
    return (
        jnp.full((head_count, query_count), NEG_LARGE, jnp.float32),
        jnp.zeros((head_count, query_count), jnp.float32),
        jnp.zeros((head_count, query_count, head_width), jnp.float32),
    )


def attend_group(state, query_group, kv_piece, key_seg, key_pos):
    query_heads, query_seg, query_pos = query_group
    head_count, query_count, head_width = query_heads.shape
    visible = (key_seg[None, :] == query_seg[:, None]) & (key_pos[None, :] <= query_pos[:, None])

    def attend_piece(current):
        running_max, running_sum, weighted_sum = current
        row_count = kv_piece.shape[0]
        key_heads = kv_piece[:, : head_count * head_width].reshape(
            row_count, head_count, head_width
        )
        value_heads = kv_piece[:, head_count * head_width :].reshape(
            row_count, head_count, head_width
        )
        scores = jnp.einsum(
            "hqe,khe->hqk", query_heads, key_heads, preferred_element_type=jnp.float32
        ) * head_width ** (-0.5)
        scores = jnp.where(visible[None], scores, NEG_LARGE)
        new_max = jnp.maximum(running_max, jnp.max(scores, axis=2))
        weights = jnp.where(visible[None], jnp.exp(scores - new_max[:, :, None]), 0.0)
        new_sum = jnp.sum(weights, axis=2)
        mixed = jnp.einsum(
            "hqk,khe->hqe",
            weights.astype(jnp.bfloat16),
            value_heads,
            preferred_element_type=jnp.float32,
        )
        return (new_max, new_sum, mixed)

    return lax.cond(jnp.any(visible), attend_piece, lambda current: current, state)


def finish(state):
    running_max, running_sum, weighted_sum = state
    return (weighted_sum / running_sum[:, :, None]).astype(jnp.bfloat16)


def write_pages(kv_rows, page_table, width_dev):
    tok_count = kv_rows.shape[0]
    block_count = tok_count // PAGE
    devices = lax.axis_size("seq")
    capacity = (block_count + devices - 1) // devices
    owner = page_table // block_count
    owner_hot = (owner[:, None] == jnp.arange(devices, dtype=jnp.int32)[None, :]).astype(jnp.int32)
    earlier = jnp.cumsum(owner_hot, axis=0) - owner_hot
    occurrence = jnp.sum(earlier * owner_hot, axis=1)
    slot = owner * capacity + occurrence
    slot_hot = slot[None, :] == jnp.arange(devices * capacity, dtype=jnp.int32)[:, None]
    flat_blocks = kv_rows.reshape(block_count, PAGE * 2 * width_dev)
    outgoing = jnp.einsum(
        "sb,bx->sx", slot_hot.astype(jnp.bfloat16), flat_blocks, preferred_element_type=jnp.float32
    ).astype(jnp.bfloat16)
    labels = jnp.sum(jnp.where(slot_hot, (page_table % block_count)[None, :] + 1, 0), axis=1) - 1
    arrived, arrived_labels = (
        lax.all_to_all(outgoing, "seq", split_axis=0, concat_axis=0, tiled=True),
        lax.all_to_all(labels, "seq", split_axis=0, concat_axis=0, tiled=True),
    )
    place_hot = (
        arrived_labels[None, :] == jnp.arange(block_count, dtype=jnp.int32)[:, None]
    ).astype(jnp.bfloat16)
    placed = jnp.einsum("bs,sx->bx", place_hot, arrived, preferred_element_type=jnp.float32).astype(
        jnp.bfloat16
    )
    placed = placed.reshape(block_count, PAGE, 2 * width_dev)
    return (placed[:, :, :width_dev], placed[:, :, width_dev:])


def body(hidden, w_qkv, w_out, seg_ids, positions, page_table):
    tok_count = hidden.shape[0]
    full_rows = lax.all_gather(hidden, "tp", axis=1, tiled=True).astype(jnp.float32)
    row_mean = jnp.mean(full_rows, axis=1, keepdims=True)
    centred = full_rows - row_mean
    row_var = jnp.mean(centred * centred, axis=1, keepdims=True)
    normed = (centred * lax.rsqrt(row_var + EPSILON)).astype(jnp.bfloat16)
    projected = jnp.einsum("td,jde->jte", normed, w_qkv, preferred_element_type=jnp.float32)
    width_dev = w_qkv.shape[2]
    heads_dev = width_dev // HEAD_DIM
    cosine, sine_part = rope_tables(positions, HEAD_DIM)
    queries = rotate(
        projected[0].reshape(tok_count, heads_dev, HEAD_DIM), cosine, sine_part
    ).astype(jnp.bfloat16)
    key_heads = rotate(
        projected[1].reshape(tok_count, heads_dev, HEAD_DIM), cosine, sine_part
    ).astype(jnp.bfloat16)
    values = projected[2].astype(jnp.bfloat16)
    kv_rows = jnp.concatenate([key_heads.reshape(tok_count, width_dev), values], axis=1)
    query_heads = jnp.transpose(queries, (1, 0, 2))
    groups = ((query_heads, seg_ids, positions),)
    states = tuple((fresh_state(query_group[0]) for query_group in groups))

    def fold_plain(fold_state, shard_piece):
        return tuple(
            (
                attend_group(one_state, query_group, shard_piece[0], shard_piece[1], shard_piece[2])
                for one_state, query_group in zip(fold_state, groups)
            )
        )

    seq_count = lax.axis_size("seq")
    int_rows = jnp.concatenate([seg_ids, positions, page_table])
    int_all = lax.all_gather(int_rows, "seq", axis=0, tiled=False)
    seg_all = int_all[:, :tok_count].reshape(-1)
    pos_all = int_all[:, tok_count : 2 * tok_count].reshape(-1)
    table_all = int_all[:, 2 * tok_count :].reshape(-1)
    kv_all = lax.all_gather(kv_rows, "seq", axis=0, tiled=True)
    states = fold_plain(states, (kv_all, seg_all, pos_all))
    block_count = tok_count // PAGE
    total_blocks = block_count * seq_count
    inverse = jnp.zeros((total_blocks,), jnp.int32).at[table_all].set(
        jnp.arange(total_blocks, dtype=jnp.int32)
    )
    mine = lax.dynamic_slice(inverse, (lax.axis_index("seq") * block_count,), (block_count,))
    placed = jnp.take(kv_all.reshape(total_blocks, PAGE, 2 * width_dev), mine, axis=0)
    k_cache = placed[:, :, :width_dev]
    v_cache = placed[:, :, width_dev:]
    finished = [finish(one_state) for one_state in states]
    attended_heads = finished[0]
    attended = jnp.transpose(attended_heads, (1, 0, 2)).reshape(tok_count, width_dev)
    partial_out = jnp.dot(attended, w_out, preferred_element_type=jnp.float32).astype(jnp.bfloat16)
    delta = lax.psum_scatter(partial_out, "tp", scatter_dimension=1, tiled=True)
    return (delta, k_cache, v_cache)


def solution(mesh):
    in_specs = (P("seq", "tp"), P(None, None, "tp"), P("tp", None), P("seq"), P("seq"), P("seq"))
    out_specs = (P("seq", "tp"), P("seq", None, "tp"), P("seq", None, "tp"))
    return jax.shard_map(body, mesh=mesh, in_specs=in_specs, out_specs=out_specs, check_vma=False)
```

```python
import jax
import jax.numpy as jnp
from jax import lax
from jax.sharding import PartitionSpec as P
from jax.experimental import pallas as pl
from jax.experimental.pallas import tpu as pltpu

HEAD_DIM = 128
PAGE = 16


ROPE_BASE = 10000.0
EPSILON = 1e-05
NEG_LARGE = -1e30


def rope_tables(position_ids, head_width):
    half_width = head_width // 2
    frequency = ROPE_BASE ** (-jnp.arange(half_width).astype(jnp.float32) * 2.0 / head_width)
    angle = position_ids.astype(jnp.float32)[:, None] * frequency[None, :]
    return (jnp.cos(angle), jnp.sin(angle))


def rotate(vectors, cosine, sine_part):
    half_width = vectors.shape[-1] // 2
    first_half = vectors[..., :half_width]
    second_half = vectors[..., half_width:]
    cos_rows = cosine[:, None, :]
    sin_rows = sine_part[:, None, :]
    return jnp.concatenate(
        [
            first_half * cos_rows - second_half * sin_rows,
            second_half * cos_rows + first_half * sin_rows,
        ],
        axis=-1,
    )


def fresh_state(query_heads):
    head_count, query_count, head_width = query_heads.shape
    return (
        jnp.full((head_count, query_count), NEG_LARGE, jnp.float32),
        jnp.zeros((head_count, query_count), jnp.float32),
        jnp.zeros((head_count, query_count, head_width), jnp.float32),
    )


def attend_group(state, query_group, kv_piece, key_seg, key_pos):
    query_heads, query_seg, query_pos = query_group
    head_count, query_count, head_width = query_heads.shape
    visible = (key_seg[None, :] == query_seg[:, None]) & (key_pos[None, :] <= query_pos[:, None])

    def attend_piece(current):
        running_max, running_sum, weighted_sum = current
        row_count = kv_piece.shape[0]
        key_heads = kv_piece[:, : head_count * head_width].reshape(
            row_count, head_count, head_width
        )
        value_heads = kv_piece[:, head_count * head_width :].reshape(
            row_count, head_count, head_width
        )
        scores = jnp.einsum(
            "hqe,khe->hqk", query_heads, key_heads, preferred_element_type=jnp.float32
        ) * head_width ** (-0.5)
        scores = jnp.where(visible[None], scores, NEG_LARGE)
        new_max = jnp.maximum(running_max, jnp.max(scores, axis=2))
        weights = jnp.where(visible[None], jnp.exp(scores - new_max[:, :, None]), 0.0)
        new_sum = jnp.sum(weights, axis=2)
        mixed = jnp.einsum(
            "hqk,khe->hqe",
            weights.astype(jnp.bfloat16),
            value_heads,
            preferred_element_type=jnp.float32,
        )
        return (new_max, new_sum, mixed)

    return lax.cond(jnp.any(visible), attend_piece, lambda current: current, state)


INTERPRET = False


def flash_kernel(need_ref, kid_ref, q_ref, k_ref, v_ref, qseg_ref, qpos_ref, kseg_ref, kpos_ref,
                 o_ref, m_scr, l_scr, acc_scr):
    j = pl.program_id(1)

    @pl.when(j == 0)
    def _():
        m_scr[...] = jnp.full(m_scr.shape, NEG_LARGE, jnp.float32)
        l_scr[...] = jnp.zeros(l_scr.shape, jnp.float32)
        acc_scr[...] = jnp.zeros(acc_scr.shape, jnp.float32)

    @pl.when(need_ref[j] != 0)
    def _():
        s = lax.dot_general(
            q_ref[...], k_ref[...], (((1,), (1,)), ((), ())), preferred_element_type=jnp.float32
        ) * HEAD_DIM ** (-0.5)
        vis = (kseg_ref[...] == qseg_ref[...]) & (kpos_ref[...] <= qpos_ref[...])
        s = jnp.where(vis, s, NEG_LARGE)
        m_prev = m_scr[...]
        m_new = jnp.maximum(m_prev, jnp.max(s, axis=1, keepdims=True))
        alpha = jnp.exp(m_prev - m_new)
        p = jnp.where(vis, jnp.exp(s - m_new), 0.0)
        l_scr[...] = alpha * l_scr[...] + jnp.sum(p, axis=1, keepdims=True)
        acc_scr[...] = alpha * acc_scr[...] + jnp.dot(
            p.astype(jnp.bfloat16), v_ref[...], preferred_element_type=jnp.float32
        )
        m_scr[...] = m_new

    @pl.when(j == pl.num_programs(1) - 1)
    def _():
        o_ref[...] = (acc_scr[...] / l_scr[...]).astype(o_ref.dtype)


def flash_attend(query_heads, seg_q, pos_q, kv_all, seg_all, pos_all):
    head_count, query_count, head_width = query_heads.shape
    key_count = kv_all.shape[0]
    block_k = query_count
    block_count = key_count // block_k
    visible = (seg_all[None, :] == seg_q[:, None]) & (pos_all[None, :] <= pos_q[:, None])
    need = jnp.any(visible.reshape(query_count, block_count, block_k), axis=(0, 2)).astype(jnp.int32)
    key_index = lax.cummax(jnp.where(need != 0, jnp.arange(block_count, dtype=jnp.int32), 0), axis=0)
    grid_spec = pltpu.PrefetchScalarGridSpec(
        num_scalar_prefetch=2,
        grid=(head_count, block_count),
        in_specs=[
            pl.BlockSpec((None, query_count, head_width), lambda h, j, nd, kd: (h, 0, 0)),
            pl.BlockSpec((block_k, head_width), lambda h, j, nd, kd: (kd[j], h)),
            pl.BlockSpec((block_k, head_width), lambda h, j, nd, kd: (kd[j], head_count + h)),
            pl.BlockSpec((query_count, 1), lambda h, j, nd, kd: (0, 0)),
            pl.BlockSpec((query_count, 1), lambda h, j, nd, kd: (0, 0)),
            pl.BlockSpec((1, block_k), lambda h, j, nd, kd: (0, kd[j])),
            pl.BlockSpec((1, block_k), lambda h, j, nd, kd: (0, kd[j])),
        ],
        out_specs=pl.BlockSpec((None, query_count, head_width), lambda h, j, nd, kd: (h, 0, 0)),
        scratch_shapes=[
            pltpu.VMEM((query_count, 1), jnp.float32),
            pltpu.VMEM((query_count, 1), jnp.float32),
            pltpu.VMEM((query_count, head_width), jnp.float32),
        ],
    )
    return pl.pallas_call(
        flash_kernel,
        grid_spec=grid_spec,
        out_shape=jax.ShapeDtypeStruct(query_heads.shape, jnp.bfloat16),
        compiler_params=pltpu.CompilerParams(dimension_semantics=("arbitrary", "arbitrary")),
        interpret=INTERPRET,
    )(
        need,
        key_index,
        query_heads,
        kv_all,
        kv_all,
        seg_q.reshape(query_count, 1),
        pos_q.reshape(query_count, 1),
        seg_all.reshape(1, key_count),
        pos_all.reshape(1, key_count),
    )


def finish(state):
    running_max, running_sum, weighted_sum = state
    return (weighted_sum / running_sum[:, :, None]).astype(jnp.bfloat16)


def write_pages(kv_rows, page_table, width_dev):
    tok_count = kv_rows.shape[0]
    block_count = tok_count // PAGE
    devices = lax.axis_size("seq")
    capacity = (block_count + devices - 1) // devices
    owner = page_table // block_count
    owner_hot = (owner[:, None] == jnp.arange(devices, dtype=jnp.int32)[None, :]).astype(jnp.int32)
    earlier = jnp.cumsum(owner_hot, axis=0) - owner_hot
    occurrence = jnp.sum(earlier * owner_hot, axis=1)
    slot = owner * capacity + occurrence
    slot_hot = slot[None, :] == jnp.arange(devices * capacity, dtype=jnp.int32)[:, None]
    flat_blocks = kv_rows.reshape(block_count, PAGE * 2 * width_dev)
    outgoing = jnp.einsum(
        "sb,bx->sx", slot_hot.astype(jnp.bfloat16), flat_blocks, preferred_element_type=jnp.float32
    ).astype(jnp.bfloat16)
    labels = jnp.sum(jnp.where(slot_hot, (page_table % block_count)[None, :] + 1, 0), axis=1) - 1
    arrived, arrived_labels = (
        lax.all_to_all(outgoing, "seq", split_axis=0, concat_axis=0, tiled=True),
        lax.all_to_all(labels, "seq", split_axis=0, concat_axis=0, tiled=True),
    )
    place_hot = (
        arrived_labels[None, :] == jnp.arange(block_count, dtype=jnp.int32)[:, None]
    ).astype(jnp.bfloat16)
    placed = jnp.einsum("bs,sx->bx", place_hot, arrived, preferred_element_type=jnp.float32).astype(
        jnp.bfloat16
    )
    placed = placed.reshape(block_count, PAGE, 2 * width_dev)
    return (placed[:, :, :width_dev], placed[:, :, width_dev:])


def body(hidden, w_qkv, w_out, seg_ids, positions, page_table):
    tok_count = hidden.shape[0]
    full_rows = lax.all_gather(hidden, "tp", axis=1, tiled=True).astype(jnp.float32)
    row_mean = jnp.mean(full_rows, axis=1, keepdims=True)
    centred = full_rows - row_mean
    row_var = jnp.mean(centred * centred, axis=1, keepdims=True)
    normed = (centred * lax.rsqrt(row_var + EPSILON)).astype(jnp.bfloat16)
    projected = jnp.einsum("td,jde->jte", normed, w_qkv, preferred_element_type=jnp.float32)
    width_dev = w_qkv.shape[2]
    heads_dev = width_dev // HEAD_DIM
    cosine, sine_part = rope_tables(positions, HEAD_DIM)
    queries = rotate(
        projected[0].reshape(tok_count, heads_dev, HEAD_DIM), cosine, sine_part
    ).astype(jnp.bfloat16)
    key_heads = rotate(
        projected[1].reshape(tok_count, heads_dev, HEAD_DIM), cosine, sine_part
    ).astype(jnp.bfloat16)
    values = projected[2].astype(jnp.bfloat16)
    kv_rows = jnp.concatenate([key_heads.reshape(tok_count, width_dev), values], axis=1)
    query_heads = jnp.transpose(queries, (1, 0, 2))
    seq_count = lax.axis_size("seq")
    int_rows = jnp.concatenate([seg_ids, positions, page_table])
    int_all = lax.all_gather(int_rows, "seq", axis=0, tiled=False)
    seg_all = int_all[:, :tok_count].reshape(-1)
    pos_all = int_all[:, tok_count : 2 * tok_count].reshape(-1)
    table_all = int_all[:, 2 * tok_count :].reshape(-1)
    kv_all = lax.all_gather(kv_rows, "seq", axis=0, tiled=True)
    attended_heads = flash_attend(query_heads, seg_ids, positions, kv_all, seg_all, pos_all)
    block_count = tok_count // PAGE
    total_blocks = block_count * seq_count
    inverse = jnp.zeros((total_blocks,), jnp.int32).at[table_all].set(
        jnp.arange(total_blocks, dtype=jnp.int32)
    )
    mine = lax.dynamic_slice(inverse, (lax.axis_index("seq") * block_count,), (block_count,))
    placed = jnp.take(kv_all.reshape(total_blocks, PAGE, 2 * width_dev), mine, axis=0)
    k_cache = placed[:, :, :width_dev]
    v_cache = placed[:, :, width_dev:]
    attended = jnp.transpose(attended_heads, (1, 0, 2)).reshape(tok_count, width_dev)
    partial_out = jnp.dot(attended, w_out, preferred_element_type=jnp.float32).astype(jnp.bfloat16)
    delta = lax.psum_scatter(partial_out, "tp", scatter_dimension=1, tiled=True)
    return (delta, k_cache, v_cache)


def solution(mesh):
    in_specs = (P("seq", "tp"), P(None, None, "tp"), P("tp", None), P("seq"), P("seq"), P("seq"))
    out_specs = (P("seq", "tp"), P("seq", None, "tp"), P("seq", None, "tp"))
    return jax.shard_map(body, mesh=mesh, in_specs=in_specs, out_specs=out_specs, check_vma=False)
```

```python
import jax
import jax.numpy as jnp
from jax import lax
from jax.sharding import PartitionSpec as P
from jax.experimental import pallas as pl
from jax.experimental.pallas import tpu as pltpu

HEAD_DIM = 128
PAGE = 16


ROPE_BASE = 10000.0
EPSILON = 1e-05
NEG_LARGE = -1e30


def rope_tables(position_ids, head_width):
    half_width = head_width // 2
    frequency = ROPE_BASE ** (-jnp.arange(half_width).astype(jnp.float32) * 2.0 / head_width)
    angle = position_ids.astype(jnp.float32)[:, None] * frequency[None, :]
    return (jnp.cos(angle), jnp.sin(angle))


def rotate(vectors, cosine, sine_part):
    half_width = vectors.shape[-1] // 2
    first_half = vectors[..., :half_width]
    second_half = vectors[..., half_width:]
    cos_rows = cosine[:, None, :]
    sin_rows = sine_part[:, None, :]
    return jnp.concatenate(
        [
            first_half * cos_rows - second_half * sin_rows,
            second_half * cos_rows + first_half * sin_rows,
        ],
        axis=-1,
    )


def fresh_state(query_heads):
    head_count, query_count, head_width = query_heads.shape
    return (
        jnp.full((head_count, query_count), NEG_LARGE, jnp.float32),
        jnp.zeros((head_count, query_count), jnp.float32),
        jnp.zeros((head_count, query_count, head_width), jnp.float32),
    )


def attend_group(state, query_group, kv_piece, key_seg, key_pos):
    query_heads, query_seg, query_pos = query_group
    head_count, query_count, head_width = query_heads.shape
    visible = (key_seg[None, :] == query_seg[:, None]) & (key_pos[None, :] <= query_pos[:, None])

    def attend_piece(current):
        running_max, running_sum, weighted_sum = current
        row_count = kv_piece.shape[0]
        key_heads = kv_piece[:, : head_count * head_width].reshape(
            row_count, head_count, head_width
        )
        value_heads = kv_piece[:, head_count * head_width :].reshape(
            row_count, head_count, head_width
        )
        scores = jnp.einsum(
            "hqe,khe->hqk", query_heads, key_heads, preferred_element_type=jnp.float32
        ) * head_width ** (-0.5)
        scores = jnp.where(visible[None], scores, NEG_LARGE)
        new_max = jnp.maximum(running_max, jnp.max(scores, axis=2))
        weights = jnp.where(visible[None], jnp.exp(scores - new_max[:, :, None]), 0.0)
        new_sum = jnp.sum(weights, axis=2)
        mixed = jnp.einsum(
            "hqk,khe->hqe",
            weights.astype(jnp.bfloat16),
            value_heads,
            preferred_element_type=jnp.float32,
        )
        return (new_max, new_sum, mixed)

    return lax.cond(jnp.any(visible), attend_piece, lambda current: current, state)


INTERPRET = False


def flash_kernel(need_ref, kid_ref, q_ref, k_ref, v_ref, qseg_ref, qpos_ref, kseg_ref, kpos_ref,
                 o_ref, m_scr, l_scr, acc_scr):
    j = pl.program_id(1)

    @pl.when(j == 0)
    def _():
        m_scr[...] = jnp.full(m_scr.shape, NEG_LARGE, jnp.float32)
        l_scr[...] = jnp.zeros(l_scr.shape, jnp.float32)
        acc_scr[...] = jnp.zeros(acc_scr.shape, jnp.float32)

    @pl.when(need_ref[j] != 0)
    def _():
        s = lax.dot_general(
            q_ref[...], k_ref[...], (((1,), (1,)), ((), ())), preferred_element_type=jnp.float32
        ) * HEAD_DIM ** (-0.5)
        vis = (kseg_ref[...] == qseg_ref[...]) & (kpos_ref[...] <= qpos_ref[...])
        s = jnp.where(vis, s, NEG_LARGE)
        m_prev = m_scr[...]
        m_new = jnp.maximum(m_prev, jnp.max(s, axis=1, keepdims=True))
        alpha = jnp.exp(m_prev - m_new)
        p = jnp.where(vis, jnp.exp(s - m_new), 0.0)
        l_scr[...] = alpha * l_scr[...] + jnp.sum(p, axis=1, keepdims=True)
        acc_scr[...] = alpha * acc_scr[...] + jnp.dot(
            p.astype(jnp.bfloat16), v_ref[...], preferred_element_type=jnp.float32
        )
        m_scr[...] = m_new

    @pl.when(j == pl.num_programs(1) - 1)
    def _():
        o_ref[...] = (acc_scr[...] / l_scr[...]).astype(o_ref.dtype)


def flash_attend(query_heads, seg_q, pos_q, kv_all, seg_all, pos_all):
    head_count, query_count, head_width = query_heads.shape
    key_count = kv_all.shape[0]
    block_k = query_count
    block_count = key_count // block_k
    visible = (seg_all[None, :] == seg_q[:, None]) & (pos_all[None, :] <= pos_q[:, None])
    need = jnp.any(visible.reshape(query_count, block_count, block_k), axis=(0, 2)).astype(jnp.int32)
    key_index = lax.cummax(jnp.where(need != 0, jnp.arange(block_count, dtype=jnp.int32), 0), axis=0)
    grid_spec = pltpu.PrefetchScalarGridSpec(
        num_scalar_prefetch=2,
        grid=(head_count, block_count),
        in_specs=[
            pl.BlockSpec((None, query_count, head_width), lambda h, j, nd, kd: (h, 0, 0)),
            pl.BlockSpec((block_k, head_width), lambda h, j, nd, kd: (kd[j], h)),
            pl.BlockSpec((block_k, head_width), lambda h, j, nd, kd: (kd[j], head_count + h)),
            pl.BlockSpec((query_count, 1), lambda h, j, nd, kd: (0, 0)),
            pl.BlockSpec((query_count, 1), lambda h, j, nd, kd: (0, 0)),
            pl.BlockSpec((1, block_k), lambda h, j, nd, kd: (0, kd[j])),
            pl.BlockSpec((1, block_k), lambda h, j, nd, kd: (0, kd[j])),
        ],
        out_specs=pl.BlockSpec((None, query_count, head_width), lambda h, j, nd, kd: (h, 0, 0)),
        scratch_shapes=[
            pltpu.VMEM((query_count, 1), jnp.float32),
            pltpu.VMEM((query_count, 1), jnp.float32),
            pltpu.VMEM((query_count, head_width), jnp.float32),
        ],
    )
    return pl.pallas_call(
        flash_kernel,
        grid_spec=grid_spec,
        out_shape=jax.ShapeDtypeStruct(query_heads.shape, jnp.bfloat16),
        compiler_params=pltpu.CompilerParams(dimension_semantics=("arbitrary", "arbitrary")),
        interpret=INTERPRET,
    )(
        need,
        key_index,
        query_heads,
        kv_all,
        kv_all,
        seg_q.reshape(query_count, 1),
        pos_q.reshape(query_count, 1),
        seg_all.reshape(1, key_count),
        pos_all.reshape(1, key_count),
    )


def finish(state):
    running_max, running_sum, weighted_sum = state
    return (weighted_sum / running_sum[:, :, None]).astype(jnp.bfloat16)


def write_pages(kv_rows, page_table, width_dev):
    tok_count = kv_rows.shape[0]
    block_count = tok_count // PAGE
    devices = lax.axis_size("seq")
    capacity = (block_count + devices - 1) // devices
    owner = page_table // block_count
    owner_hot = (owner[:, None] == jnp.arange(devices, dtype=jnp.int32)[None, :]).astype(jnp.int32)
    earlier = jnp.cumsum(owner_hot, axis=0) - owner_hot
    occurrence = jnp.sum(earlier * owner_hot, axis=1)
    slot = owner * capacity + occurrence
    slot_hot = slot[None, :] == jnp.arange(devices * capacity, dtype=jnp.int32)[:, None]
    flat_blocks = kv_rows.reshape(block_count, PAGE * 2 * width_dev)
    outgoing = jnp.einsum(
        "sb,bx->sx", slot_hot.astype(jnp.bfloat16), flat_blocks, preferred_element_type=jnp.float32
    ).astype(jnp.bfloat16)
    labels = jnp.sum(jnp.where(slot_hot, (page_table % block_count)[None, :] + 1, 0), axis=1) - 1
    arrived, arrived_labels = (
        lax.all_to_all(outgoing, "seq", split_axis=0, concat_axis=0, tiled=True),
        lax.all_to_all(labels, "seq", split_axis=0, concat_axis=0, tiled=True),
    )
    place_hot = (
        arrived_labels[None, :] == jnp.arange(block_count, dtype=jnp.int32)[:, None]
    ).astype(jnp.bfloat16)
    placed = jnp.einsum("bs,sx->bx", place_hot, arrived, preferred_element_type=jnp.float32).astype(
        jnp.bfloat16
    )
    placed = placed.reshape(block_count, PAGE, 2 * width_dev)
    return (placed[:, :, :width_dev], placed[:, :, width_dev:])


def body(hidden, w_qkv, w_out, seg_ids, positions, page_table):
    tok_count = hidden.shape[0]
    full_rows = lax.all_gather(hidden, "tp", axis=1, tiled=True).astype(jnp.float32)
    row_mean = jnp.mean(full_rows, axis=1, keepdims=True)
    centred = full_rows - row_mean
    row_var = jnp.mean(centred * centred, axis=1, keepdims=True)
    normed = (centred * lax.rsqrt(row_var + EPSILON)).astype(jnp.bfloat16)
    projected = jnp.einsum("td,jde->jte", normed, w_qkv, preferred_element_type=jnp.float32)
    width_dev = w_qkv.shape[2]
    heads_dev = width_dev // HEAD_DIM
    cosine, sine_part = rope_tables(positions, HEAD_DIM)
    queries = rotate(
        projected[0].reshape(tok_count, heads_dev, HEAD_DIM), cosine, sine_part
    ).astype(jnp.bfloat16)
    key_heads = rotate(
        projected[1].reshape(tok_count, heads_dev, HEAD_DIM), cosine, sine_part
    ).astype(jnp.bfloat16)
    values = projected[2].astype(jnp.bfloat16)
    kv_rows = jnp.concatenate([key_heads.reshape(tok_count, width_dev), values], axis=1)
    query_heads = jnp.transpose(queries, (1, 0, 2))
    seq_count = lax.axis_size("seq")
    table_rows = jnp.repeat(page_table, PAGE)
    side = jnp.stack(
        [seg_ids, positions // 128, positions % 128, table_rows // 128, table_rows % 128], axis=1
    )
    side = jnp.pad(side, ((0, 0), (0, 128 - side.shape[1]))).astype(jnp.bfloat16)
    kv_all = lax.all_gather(jnp.concatenate([kv_rows, side], axis=1), "seq", axis=0, tiled=True)
    side_all = kv_all[:, 2 * width_dev : 2 * width_dev + 5].astype(jnp.int32)
    seg_all = side_all[:, 0]
    pos_all = side_all[:, 1] * 128 + side_all[:, 2]
    table_all = (side_all[:, 3] * 128 + side_all[:, 4])[::PAGE]
    attended_heads = flash_attend(query_heads, seg_ids, positions, kv_all, seg_all, pos_all)
    block_count = tok_count // PAGE
    total_blocks = block_count * seq_count
    inverse = jnp.zeros((total_blocks,), jnp.int32).at[table_all].set(
        jnp.arange(total_blocks, dtype=jnp.int32)
    )
    mine = lax.dynamic_slice(inverse, (lax.axis_index("seq") * block_count,), (block_count,))
    placed = jnp.take(kv_all.reshape(total_blocks, PAGE, kv_all.shape[1]), mine, axis=0)
    k_cache = placed[:, :, :width_dev]
    v_cache = placed[:, :, width_dev : 2 * width_dev]
    attended = jnp.transpose(attended_heads, (1, 0, 2)).reshape(tok_count, width_dev)
    partial_out = jnp.dot(attended, w_out, preferred_element_type=jnp.float32).astype(jnp.bfloat16)
    delta = lax.psum_scatter(partial_out, "tp", scatter_dimension=1, tiled=True)
    return (delta, k_cache, v_cache)


def solution(mesh):
    in_specs = (P("seq", "tp"), P(None, None, "tp"), P("tp", None), P("seq"), P("seq"), P("seq"))
    out_specs = (P("seq", "tp"), P("seq", None, "tp"), P("seq", None, "tp"))
    return jax.shard_map(body, mesh=mesh, in_specs=in_specs, out_specs=out_specs, check_vma=False)
```

```python
import jax
import jax.numpy as jnp
from jax import lax
from jax.sharding import PartitionSpec as P
from jax.experimental import pallas as pl
from jax.experimental.pallas import tpu as pltpu

HEAD_DIM = 128
PAGE = 16


ROPE_BASE = 10000.0
EPSILON = 1e-05
NEG_LARGE = -1e30


def rope_tables(position_ids, head_width):
    half_width = head_width // 2
    frequency = ROPE_BASE ** (-jnp.arange(half_width).astype(jnp.float32) * 2.0 / head_width)
    angle = position_ids.astype(jnp.float32)[:, None] * frequency[None, :]
    return (jnp.cos(angle), jnp.sin(angle))


def rotate(vectors, cosine, sine_part):
    half_width = vectors.shape[-1] // 2
    first_half = vectors[..., :half_width]
    second_half = vectors[..., half_width:]
    cos_rows = cosine[:, None, :]
    sin_rows = sine_part[:, None, :]
    return jnp.concatenate(
        [
            first_half * cos_rows - second_half * sin_rows,
            second_half * cos_rows + first_half * sin_rows,
        ],
        axis=-1,
    )


def fresh_state(query_heads):
    head_count, query_count, head_width = query_heads.shape
    return (
        jnp.full((head_count, query_count), NEG_LARGE, jnp.float32),
        jnp.zeros((head_count, query_count), jnp.float32),
        jnp.zeros((head_count, query_count, head_width), jnp.float32),
    )


def attend_group(state, query_group, kv_piece, key_seg, key_pos):
    query_heads, query_seg, query_pos = query_group
    head_count, query_count, head_width = query_heads.shape
    visible = (key_seg[None, :] == query_seg[:, None]) & (key_pos[None, :] <= query_pos[:, None])

    def attend_piece(current):
        running_max, running_sum, weighted_sum = current
        row_count = kv_piece.shape[0]
        key_heads = kv_piece[:, : head_count * head_width].reshape(
            row_count, head_count, head_width
        )
        value_heads = kv_piece[:, head_count * head_width :].reshape(
            row_count, head_count, head_width
        )
        scores = jnp.einsum(
            "hqe,khe->hqk", query_heads, key_heads, preferred_element_type=jnp.float32
        ) * head_width ** (-0.5)
        scores = jnp.where(visible[None], scores, NEG_LARGE)
        new_max = jnp.maximum(running_max, jnp.max(scores, axis=2))
        weights = jnp.where(visible[None], jnp.exp(scores - new_max[:, :, None]), 0.0)
        new_sum = jnp.sum(weights, axis=2)
        mixed = jnp.einsum(
            "hqk,khe->hqe",
            weights.astype(jnp.bfloat16),
            value_heads,
            preferred_element_type=jnp.float32,
        )
        return (new_max, new_sum, mixed)

    return lax.cond(jnp.any(visible), attend_piece, lambda current: current, state)


INTERPRET = False


def flash_kernel(need_ref, kid_ref, q_ref, k_ref, v_ref, qseg_ref, qpos_ref, kseg_ref, kpos_ref,
                 o_ref, m_scr, l_scr, acc_scr):
    j = pl.program_id(0)
    head_count, _, head_width = q_ref.shape

    @pl.when(j == 0)
    def _():
        m_scr[...] = jnp.full(m_scr.shape, NEG_LARGE, jnp.float32)
        l_scr[...] = jnp.zeros(l_scr.shape, jnp.float32)
        acc_scr[...] = jnp.zeros(acc_scr.shape, jnp.float32)

    @pl.when(need_ref[j] != 0)
    def _():
        vis = (kseg_ref[...] == qseg_ref[...]) & (kpos_ref[...] <= qpos_ref[...])
        for h in range(head_count):
            cols = slice(h * head_width, (h + 1) * head_width)
            s = lax.dot_general(
                q_ref[h], k_ref[:, cols], (((1,), (1,)), ((), ())),
                preferred_element_type=jnp.float32,
            ) * HEAD_DIM ** (-0.5)
            s = jnp.where(vis, s, NEG_LARGE)
            m_prev = m_scr[h]
            m_new = jnp.maximum(m_prev, jnp.max(s, axis=1, keepdims=True))
            alpha = jnp.exp(m_prev - m_new)
            p = jnp.exp(s - m_new)
            l_scr[h] = alpha * l_scr[h] + jnp.sum(p, axis=1, keepdims=True)
            acc_scr[h] = alpha * acc_scr[h] + jnp.dot(
                p.astype(jnp.bfloat16), v_ref[:, cols], preferred_element_type=jnp.float32
            )
            m_scr[h] = m_new

    @pl.when(j == pl.num_programs(0) - 1)
    def _():
        o_ref[...] = (acc_scr[...] / l_scr[...]).astype(o_ref.dtype)


def flash_attend(query_heads, seg_q, pos_q, kv_all, seg_all, pos_all):
    head_count, query_count, head_width = query_heads.shape
    key_count = kv_all.shape[0]
    width_dev = head_count * head_width
    block_k = query_count
    block_count = key_count // block_k
    visible = (seg_all[None, :] == seg_q[:, None]) & (pos_all[None, :] <= pos_q[:, None])
    need = jnp.any(visible.reshape(query_count, block_count, block_k), axis=(0, 2)).astype(jnp.int32)
    key_index = lax.cummax(jnp.where(need != 0, jnp.arange(block_count, dtype=jnp.int32), 0), axis=0)
    grid_spec = pltpu.PrefetchScalarGridSpec(
        num_scalar_prefetch=2,
        grid=(block_count,),
        in_specs=[
            pl.BlockSpec((head_count, query_count, head_width), lambda j, nd, kd: (0, 0, 0)),
            pl.BlockSpec((block_k, width_dev), lambda j, nd, kd: (kd[j], 0)),
            pl.BlockSpec((block_k, width_dev), lambda j, nd, kd: (kd[j], 1)),
            pl.BlockSpec((query_count, 1), lambda j, nd, kd: (0, 0)),
            pl.BlockSpec((query_count, 1), lambda j, nd, kd: (0, 0)),
            pl.BlockSpec((1, block_k), lambda j, nd, kd: (0, kd[j])),
            pl.BlockSpec((1, block_k), lambda j, nd, kd: (0, kd[j])),
        ],
        out_specs=pl.BlockSpec((head_count, query_count, head_width), lambda j, nd, kd: (0, 0, 0)),
        scratch_shapes=[
            pltpu.VMEM((head_count, query_count, 1), jnp.float32),
            pltpu.VMEM((head_count, query_count, 1), jnp.float32),
            pltpu.VMEM((head_count, query_count, head_width), jnp.float32),
        ],
    )
    return pl.pallas_call(
        flash_kernel,
        grid_spec=grid_spec,
        out_shape=jax.ShapeDtypeStruct(query_heads.shape, jnp.bfloat16),
        compiler_params=pltpu.CompilerParams(dimension_semantics=("arbitrary",)),
        interpret=INTERPRET,
    )(
        need,
        key_index,
        query_heads,
        kv_all,
        kv_all,
        seg_q.reshape(query_count, 1),
        pos_q.reshape(query_count, 1),
        seg_all.reshape(1, key_count),
        pos_all.reshape(1, key_count),
    )


def finish(state):
    running_max, running_sum, weighted_sum = state
    return (weighted_sum / running_sum[:, :, None]).astype(jnp.bfloat16)


def write_pages(kv_rows, page_table, width_dev):
    tok_count = kv_rows.shape[0]
    block_count = tok_count // PAGE
    devices = lax.axis_size("seq")
    capacity = (block_count + devices - 1) // devices
    owner = page_table // block_count
    owner_hot = (owner[:, None] == jnp.arange(devices, dtype=jnp.int32)[None, :]).astype(jnp.int32)
    earlier = jnp.cumsum(owner_hot, axis=0) - owner_hot
    occurrence = jnp.sum(earlier * owner_hot, axis=1)
    slot = owner * capacity + occurrence
    slot_hot = slot[None, :] == jnp.arange(devices * capacity, dtype=jnp.int32)[:, None]
    flat_blocks = kv_rows.reshape(block_count, PAGE * 2 * width_dev)
    outgoing = jnp.einsum(
        "sb,bx->sx", slot_hot.astype(jnp.bfloat16), flat_blocks, preferred_element_type=jnp.float32
    ).astype(jnp.bfloat16)
    labels = jnp.sum(jnp.where(slot_hot, (page_table % block_count)[None, :] + 1, 0), axis=1) - 1
    arrived, arrived_labels = (
        lax.all_to_all(outgoing, "seq", split_axis=0, concat_axis=0, tiled=True),
        lax.all_to_all(labels, "seq", split_axis=0, concat_axis=0, tiled=True),
    )
    place_hot = (
        arrived_labels[None, :] == jnp.arange(block_count, dtype=jnp.int32)[:, None]
    ).astype(jnp.bfloat16)
    placed = jnp.einsum("bs,sx->bx", place_hot, arrived, preferred_element_type=jnp.float32).astype(
        jnp.bfloat16
    )
    placed = placed.reshape(block_count, PAGE, 2 * width_dev)
    return (placed[:, :, :width_dev], placed[:, :, width_dev:])


def body(hidden, w_qkv, w_out, seg_ids, positions, page_table):
    tok_count = hidden.shape[0]
    full_rows = lax.all_gather(hidden, "tp", axis=1, tiled=True).astype(jnp.float32)
    row_mean = jnp.mean(full_rows, axis=1, keepdims=True)
    centred = full_rows - row_mean
    row_var = jnp.mean(centred * centred, axis=1, keepdims=True)
    normed = (centred * lax.rsqrt(row_var + EPSILON)).astype(jnp.bfloat16)
    projected = jnp.einsum("td,jde->jte", normed, w_qkv, preferred_element_type=jnp.float32)
    width_dev = w_qkv.shape[2]
    heads_dev = width_dev // HEAD_DIM
    cosine, sine_part = rope_tables(positions, HEAD_DIM)
    queries = rotate(
        projected[0].reshape(tok_count, heads_dev, HEAD_DIM), cosine, sine_part
    ).astype(jnp.bfloat16)
    key_heads = rotate(
        projected[1].reshape(tok_count, heads_dev, HEAD_DIM), cosine, sine_part
    ).astype(jnp.bfloat16)
    values = projected[2].astype(jnp.bfloat16)
    kv_rows = jnp.concatenate([key_heads.reshape(tok_count, width_dev), values], axis=1)
    query_heads = jnp.transpose(queries, (1, 0, 2))
    seq_count = lax.axis_size("seq")
    int_rows = jnp.concatenate([seg_ids, positions, page_table])
    int_all = lax.all_gather(int_rows, "seq", axis=0, tiled=False)
    seg_all = int_all[:, :tok_count].reshape(-1)
    pos_all = int_all[:, tok_count : 2 * tok_count].reshape(-1)
    table_all = int_all[:, 2 * tok_count :].reshape(-1)
    kv_all = lax.all_gather(kv_rows, "seq", axis=0, tiled=True)
    attended_heads = flash_attend(query_heads, seg_ids, positions, kv_all, seg_all, pos_all)
    block_count = tok_count // PAGE
    total_blocks = block_count * seq_count
    inverse = jnp.zeros((total_blocks,), jnp.int32).at[table_all].set(
        jnp.arange(total_blocks, dtype=jnp.int32)
    )
    mine = lax.dynamic_slice(inverse, (lax.axis_index("seq") * block_count,), (block_count,))
    placed = jnp.take(kv_all.reshape(total_blocks, PAGE, 2 * width_dev), mine, axis=0)
    k_cache = placed[:, :, :width_dev]
    v_cache = placed[:, :, width_dev:]
    attended = jnp.transpose(attended_heads, (1, 0, 2)).reshape(tok_count, width_dev)
    partial_out = jnp.dot(attended, w_out, preferred_element_type=jnp.float32).astype(jnp.bfloat16)
    delta = lax.psum_scatter(partial_out, "tp", scatter_dimension=1, tiled=True)
    return (delta, k_cache, v_cache)


def solution(mesh):
    in_specs = (P("seq", "tp"), P(None, None, "tp"), P("tp", None), P("seq"), P("seq"), P("seq"))
    out_specs = (P("seq", "tp"), P("seq", None, "tp"), P("seq", None, "tp"))
    return jax.shard_map(body, mesh=mesh, in_specs=in_specs, out_specs=out_specs, check_vma=False)
```

```python
import jax
import jax.numpy as jnp
from jax import lax
from jax.sharding import PartitionSpec as P
from jax.experimental import pallas as pl
from jax.experimental.pallas import tpu as pltpu

HEAD_DIM = 128
PAGE = 16


ROPE_BASE = 10000.0
EPSILON = 1e-05
NEG_LARGE = -1e30


def rope_tables(position_ids, head_width):
    half_width = head_width // 2
    frequency = ROPE_BASE ** (-jnp.arange(half_width).astype(jnp.float32) * 2.0 / head_width)
    angle = position_ids.astype(jnp.float32)[:, None] * frequency[None, :]
    return (jnp.cos(angle), jnp.sin(angle))


def rotate(vectors, cosine, sine_part):
    half_width = vectors.shape[-1] // 2
    first_half = vectors[..., :half_width]
    second_half = vectors[..., half_width:]
    cos_rows = cosine[:, None, :]
    sin_rows = sine_part[:, None, :]
    return jnp.concatenate(
        [
            first_half * cos_rows - second_half * sin_rows,
            second_half * cos_rows + first_half * sin_rows,
        ],
        axis=-1,
    )


def fresh_state(query_heads):
    head_count, query_count, head_width = query_heads.shape
    return (
        jnp.full((head_count, query_count), NEG_LARGE, jnp.float32),
        jnp.zeros((head_count, query_count), jnp.float32),
        jnp.zeros((head_count, query_count, head_width), jnp.float32),
    )


def attend_group(state, query_group, kv_piece, key_seg, key_pos):
    query_heads, query_seg, query_pos = query_group
    head_count, query_count, head_width = query_heads.shape
    visible = (key_seg[None, :] == query_seg[:, None]) & (key_pos[None, :] <= query_pos[:, None])

    def attend_piece(current):
        running_max, running_sum, weighted_sum = current
        row_count = kv_piece.shape[0]
        key_heads = kv_piece[:, : head_count * head_width].reshape(
            row_count, head_count, head_width
        )
        value_heads = kv_piece[:, head_count * head_width :].reshape(
            row_count, head_count, head_width
        )
        scores = jnp.einsum(
            "hqe,khe->hqk", query_heads, key_heads, preferred_element_type=jnp.float32
        ) * head_width ** (-0.5)
        scores = jnp.where(visible[None], scores, NEG_LARGE)
        new_max = jnp.maximum(running_max, jnp.max(scores, axis=2))
        weights = jnp.where(visible[None], jnp.exp(scores - new_max[:, :, None]), 0.0)
        new_sum = jnp.sum(weights, axis=2)
        mixed = jnp.einsum(
            "hqk,khe->hqe",
            weights.astype(jnp.bfloat16),
            value_heads,
            preferred_element_type=jnp.float32,
        )
        return (new_max, new_sum, mixed)

    return lax.cond(jnp.any(visible), attend_piece, lambda current: current, state)


INTERPRET = False


def flash_kernel(need_ref, kid_ref, q_ref, k_ref, v_ref, qseg_ref, qpos_ref, kseg_ref, kpos_ref,
                 o_ref, m_scr, l_scr, acc_scr):
    j = pl.program_id(0)
    head_count, _, head_width = q_ref.shape

    @pl.when(j == 0)
    def _():
        m_scr[...] = jnp.full(m_scr.shape, NEG_LARGE, jnp.float32)
        l_scr[...] = jnp.zeros(l_scr.shape, jnp.float32)
        acc_scr[...] = jnp.zeros(acc_scr.shape, jnp.float32)

    @pl.when(need_ref[j] != 0)
    def _():
        vis = (kseg_ref[...] == qseg_ref[...]) & (kpos_ref[...] <= qpos_ref[...])
        for h in range(head_count):
            cols = slice(h * head_width, (h + 1) * head_width)
            s = lax.dot_general(
                q_ref[h], k_ref[:, cols], (((1,), (1,)), ((), ())),
                preferred_element_type=jnp.float32,
            ) * HEAD_DIM ** (-0.5)
            s = jnp.where(vis, s, NEG_LARGE)
            m_prev = m_scr[h]
            m_new = jnp.maximum(m_prev, jnp.max(s, axis=1, keepdims=True))
            alpha = jnp.exp(m_prev - m_new)
            p = jnp.exp(s - m_new)
            l_scr[h] = alpha * l_scr[h] + jnp.sum(p, axis=1, keepdims=True)
            acc_scr[h] = alpha * acc_scr[h] + jnp.dot(
                p.astype(jnp.bfloat16), v_ref[:, cols], preferred_element_type=jnp.float32
            )
            m_scr[h] = m_new

    @pl.when(j == pl.num_programs(0) - 1)
    def _():
        o_ref[...] = (acc_scr[...] / l_scr[...]).astype(o_ref.dtype)


def flash_attend(query_heads, seg_q, pos_q, kv_all, seg_all, pos_all):
    head_count, query_count, head_width = query_heads.shape
    key_count = kv_all.shape[0]
    width_dev = head_count * head_width
    block_k = query_count
    block_count = key_count // block_k
    visible = (seg_all[None, :] == seg_q[:, None]) & (pos_all[None, :] <= pos_q[:, None])
    need = jnp.any(visible.reshape(query_count, block_count, block_k), axis=(0, 2)).astype(jnp.int32)
    key_index = lax.cummax(jnp.where(need != 0, jnp.arange(block_count, dtype=jnp.int32), 0), axis=0)
    grid_spec = pltpu.PrefetchScalarGridSpec(
        num_scalar_prefetch=2,
        grid=(block_count,),
        in_specs=[
            pl.BlockSpec((head_count, query_count, head_width), lambda j, nd, kd: (0, 0, 0)),
            pl.BlockSpec((block_k, width_dev), lambda j, nd, kd: (kd[j], 0)),
            pl.BlockSpec((block_k, width_dev), lambda j, nd, kd: (kd[j], 1)),
            pl.BlockSpec((query_count, 1), lambda j, nd, kd: (0, 0)),
            pl.BlockSpec((query_count, 1), lambda j, nd, kd: (0, 0)),
            pl.BlockSpec((1, block_k), lambda j, nd, kd: (0, kd[j])),
            pl.BlockSpec((1, block_k), lambda j, nd, kd: (0, kd[j])),
        ],
        out_specs=pl.BlockSpec((head_count, query_count, head_width), lambda j, nd, kd: (0, 0, 0)),
        scratch_shapes=[
            pltpu.VMEM((head_count, query_count, 1), jnp.float32),
            pltpu.VMEM((head_count, query_count, 1), jnp.float32),
            pltpu.VMEM((head_count, query_count, head_width), jnp.float32),
        ],
    )
    return pl.pallas_call(
        flash_kernel,
        grid_spec=grid_spec,
        out_shape=jax.ShapeDtypeStruct(query_heads.shape, jnp.bfloat16),
        compiler_params=pltpu.CompilerParams(dimension_semantics=("arbitrary",)),
        interpret=INTERPRET,
    )(
        need,
        key_index,
        query_heads,
        kv_all,
        kv_all,
        seg_q.reshape(query_count, 1),
        pos_q.reshape(query_count, 1),
        seg_all.reshape(1, key_count),
        pos_all.reshape(1, key_count),
    )


def finish(state):
    running_max, running_sum, weighted_sum = state
    return (weighted_sum / running_sum[:, :, None]).astype(jnp.bfloat16)


def write_pages(kv_rows, page_table, width_dev):
    tok_count = kv_rows.shape[0]
    block_count = tok_count // PAGE
    devices = lax.axis_size("seq")
    capacity = (block_count + devices - 1) // devices
    owner = page_table // block_count
    owner_hot = (owner[:, None] == jnp.arange(devices, dtype=jnp.int32)[None, :]).astype(jnp.int32)
    earlier = jnp.cumsum(owner_hot, axis=0) - owner_hot
    occurrence = jnp.sum(earlier * owner_hot, axis=1)
    slot = owner * capacity + occurrence
    slot_hot = slot[None, :] == jnp.arange(devices * capacity, dtype=jnp.int32)[:, None]
    flat_blocks = kv_rows.reshape(block_count, PAGE * 2 * width_dev)
    outgoing = jnp.einsum(
        "sb,bx->sx", slot_hot.astype(jnp.bfloat16), flat_blocks, preferred_element_type=jnp.float32
    ).astype(jnp.bfloat16)
    labels = jnp.sum(jnp.where(slot_hot, (page_table % block_count)[None, :] + 1, 0), axis=1) - 1
    arrived, arrived_labels = (
        lax.all_to_all(outgoing, "seq", split_axis=0, concat_axis=0, tiled=True),
        lax.all_to_all(labels, "seq", split_axis=0, concat_axis=0, tiled=True),
    )
    place_hot = (
        arrived_labels[None, :] == jnp.arange(block_count, dtype=jnp.int32)[:, None]
    ).astype(jnp.bfloat16)
    placed = jnp.einsum("bs,sx->bx", place_hot, arrived, preferred_element_type=jnp.float32).astype(
        jnp.bfloat16
    )
    placed = placed.reshape(block_count, PAGE, 2 * width_dev)
    return (placed[:, :, :width_dev], placed[:, :, width_dev:])


def body(hidden, w_qkv, w_out, seg_ids, positions, page_table):
    tok_count = hidden.shape[0]
    full_rows = lax.all_gather(hidden, "tp", axis=1, tiled=True).astype(jnp.float32)
    row_mean = jnp.mean(full_rows, axis=1, keepdims=True)
    centred = full_rows - row_mean
    row_var = jnp.mean(centred * centred, axis=1, keepdims=True)
    normed = (centred * lax.rsqrt(row_var + EPSILON)).astype(jnp.bfloat16)
    projected = jnp.einsum("td,jde->jte", normed, w_qkv, preferred_element_type=jnp.float32)
    width_dev = w_qkv.shape[2]
    heads_dev = width_dev // HEAD_DIM
    cosine, sine_part = rope_tables(positions, HEAD_DIM)
    queries = rotate(
        projected[0].reshape(tok_count, heads_dev, HEAD_DIM), cosine, sine_part
    ).astype(jnp.bfloat16)
    key_heads = rotate(
        projected[1].reshape(tok_count, heads_dev, HEAD_DIM), cosine, sine_part
    ).astype(jnp.bfloat16)
    values = projected[2].astype(jnp.bfloat16)
    kv_rows = jnp.concatenate([key_heads.reshape(tok_count, width_dev), values], axis=1)
    query_heads = jnp.transpose(queries, (1, 0, 2))
    seq_count = lax.axis_size("seq")
    int_rows = jnp.concatenate([seg_ids, positions, page_table])
    int_all = lax.all_gather(int_rows, "seq", axis=0, tiled=False)
    seg_all = int_all[:, :tok_count].reshape(-1)
    pos_all = int_all[:, tok_count : 2 * tok_count].reshape(-1)
    table_all = int_all[:, 2 * tok_count :].reshape(-1)
    kv_all = lax.all_gather(kv_rows, "seq", axis=0, tiled=True)
    attended_heads = flash_attend(query_heads, seg_ids, positions, kv_all, seg_all, pos_all)
    block_count = tok_count // PAGE
    total_blocks = block_count * seq_count
    inverse = jnp.zeros((total_blocks,), jnp.int32).at[table_all].set(
        jnp.arange(total_blocks, dtype=jnp.int32)
    )
    mine = lax.dynamic_slice(inverse, (lax.axis_index("seq") * block_count,), (block_count,))
    placed = jnp.take(kv_all.reshape(total_blocks, PAGE, 2 * width_dev), mine, axis=0)
    k_cache = placed[:, :, :width_dev]
    v_cache = placed[:, :, width_dev:]
    attended = jnp.transpose(attended_heads, (1, 0, 2)).reshape(tok_count, width_dev)
    partial_out = jnp.dot(attended, w_out, preferred_element_type=jnp.float32).astype(jnp.bfloat16)
    tp_count = lax.axis_size("tp")
    pieces = lax.all_to_all(
        partial_out.reshape(tok_count, tp_count, -1), "tp", split_axis=1, concat_axis=1, tiled=True
    )
    delta = jnp.sum(pieces.astype(jnp.float32), axis=1).astype(jnp.bfloat16)
    return (delta, k_cache, v_cache)


def solution(mesh):
    in_specs = (P("seq", "tp"), P(None, None, "tp"), P("tp", None), P("seq"), P("seq"), P("seq"))
    out_specs = (P("seq", "tp"), P("seq", None, "tp"), P("seq", None, "tp"))
    return jax.shard_map(body, mesh=mesh, in_specs=in_specs, out_specs=out_specs, check_vma=False)
```

```python
import jax
import jax.numpy as jnp
from jax import lax
from jax.sharding import PartitionSpec as P
from jax.experimental import pallas as pl
from jax.experimental.pallas import tpu as pltpu

HEAD_DIM = 128
PAGE = 16


ROPE_BASE = 10000.0
EPSILON = 1e-05
NEG_LARGE = -1e30


def rope_tables(position_ids, head_width):
    half_width = head_width // 2
    frequency = ROPE_BASE ** (-jnp.arange(half_width).astype(jnp.float32) * 2.0 / head_width)
    angle = position_ids.astype(jnp.float32)[:, None] * frequency[None, :]
    return (jnp.cos(angle), jnp.sin(angle))


def rotate(vectors, cosine, sine_part):
    half_width = vectors.shape[-1] // 2
    first_half = vectors[..., :half_width]
    second_half = vectors[..., half_width:]
    cos_rows = cosine[:, None, :]
    sin_rows = sine_part[:, None, :]
    return jnp.concatenate(
        [
            first_half * cos_rows - second_half * sin_rows,
            second_half * cos_rows + first_half * sin_rows,
        ],
        axis=-1,
    )


def fresh_state(query_heads):
    head_count, query_count, head_width = query_heads.shape
    return (
        jnp.full((head_count, query_count), NEG_LARGE, jnp.float32),
        jnp.zeros((head_count, query_count), jnp.float32),
        jnp.zeros((head_count, query_count, head_width), jnp.float32),
    )


def attend_group(state, query_group, kv_piece, key_seg, key_pos):
    query_heads, query_seg, query_pos = query_group
    head_count, query_count, head_width = query_heads.shape
    visible = (key_seg[None, :] == query_seg[:, None]) & (key_pos[None, :] <= query_pos[:, None])

    def attend_piece(current):
        running_max, running_sum, weighted_sum = current
        row_count = kv_piece.shape[0]
        key_heads = kv_piece[:, : head_count * head_width].reshape(
            row_count, head_count, head_width
        )
        value_heads = kv_piece[:, head_count * head_width :].reshape(
            row_count, head_count, head_width
        )
        scores = jnp.einsum(
            "hqe,khe->hqk", query_heads, key_heads, preferred_element_type=jnp.float32
        ) * head_width ** (-0.5)
        scores = jnp.where(visible[None], scores, NEG_LARGE)
        new_max = jnp.maximum(running_max, jnp.max(scores, axis=2))
        weights = jnp.where(visible[None], jnp.exp(scores - new_max[:, :, None]), 0.0)
        new_sum = jnp.sum(weights, axis=2)
        mixed = jnp.einsum(
            "hqk,khe->hqe",
            weights.astype(jnp.bfloat16),
            value_heads,
            preferred_element_type=jnp.float32,
        )
        return (new_max, new_sum, mixed)

    return lax.cond(jnp.any(visible), attend_piece, lambda current: current, state)


INTERPRET = False


def flash_kernel(need_ref, kid_ref, q_ref, k_ref, v_ref, qseg_ref, qpos_ref, kseg_ref, kpos_ref,
                 o_ref, m_scr, l_scr, acc_scr):
    j = pl.program_id(0)
    head_count, _, head_width = q_ref.shape

    @pl.when(j == 0)
    def _():
        m_scr[...] = jnp.full(m_scr.shape, NEG_LARGE, jnp.float32)
        l_scr[...] = jnp.zeros(l_scr.shape, jnp.float32)
        acc_scr[...] = jnp.zeros(acc_scr.shape, jnp.float32)

    @pl.when(need_ref[j] != 0)
    def _():
        vis = (kseg_ref[...] == qseg_ref[...]) & (kpos_ref[...] <= qpos_ref[...])
        for h in range(head_count):
            cols = slice(h * head_width, (h + 1) * head_width)
            s = lax.dot_general(
                q_ref[h], k_ref[:, cols], (((1,), (1,)), ((), ())),
                preferred_element_type=jnp.float32,
            ) * HEAD_DIM ** (-0.5)
            s = jnp.where(vis, s, NEG_LARGE)
            m_prev = m_scr[h]
            m_new = jnp.maximum(m_prev, jnp.max(s, axis=1, keepdims=True))
            alpha = jnp.exp(m_prev - m_new)
            p = jnp.exp(s - m_new)
            l_scr[h] = alpha * l_scr[h] + jnp.sum(p, axis=1, keepdims=True)
            acc_scr[h] = alpha * acc_scr[h] + jnp.dot(
                p.astype(jnp.bfloat16), v_ref[:, cols], preferred_element_type=jnp.float32
            )
            m_scr[h] = m_new

    @pl.when(j == pl.num_programs(0) - 1)
    def _():
        o_ref[...] = (acc_scr[...] / l_scr[...]).astype(o_ref.dtype)


def flash_attend(query_heads, seg_q, pos_q, kv_all, seg_all, pos_all):
    head_count, query_count, head_width = query_heads.shape
    key_count = kv_all.shape[0]
    width_dev = head_count * head_width
    block_k = query_count
    block_count = key_count // block_k
    seg_blocks = seg_all.reshape(block_count, block_k)
    pos_low = jnp.min(pos_all.reshape(block_count, block_k), axis=1)
    need = (
        (jnp.min(seg_blocks, axis=1) <= jnp.max(seg_q))
        & (jnp.max(seg_blocks, axis=1) >= jnp.min(seg_q))
        & (pos_low <= jnp.max(pos_q))
    ).astype(jnp.int32)
    key_index = lax.cummax(jnp.where(need != 0, jnp.arange(block_count, dtype=jnp.int32), 0), axis=0)
    grid_spec = pltpu.PrefetchScalarGridSpec(
        num_scalar_prefetch=2,
        grid=(block_count,),
        in_specs=[
            pl.BlockSpec((head_count, query_count, head_width), lambda j, nd, kd: (0, 0, 0)),
            pl.BlockSpec((block_k, width_dev), lambda j, nd, kd: (kd[j], 0)),
            pl.BlockSpec((block_k, width_dev), lambda j, nd, kd: (kd[j], 1)),
            pl.BlockSpec((query_count, 1), lambda j, nd, kd: (0, 0)),
            pl.BlockSpec((query_count, 1), lambda j, nd, kd: (0, 0)),
            pl.BlockSpec((1, block_k), lambda j, nd, kd: (0, kd[j])),
            pl.BlockSpec((1, block_k), lambda j, nd, kd: (0, kd[j])),
        ],
        out_specs=pl.BlockSpec((head_count, query_count, head_width), lambda j, nd, kd: (0, 0, 0)),
        scratch_shapes=[
            pltpu.VMEM((head_count, query_count, 1), jnp.float32),
            pltpu.VMEM((head_count, query_count, 1), jnp.float32),
            pltpu.VMEM((head_count, query_count, head_width), jnp.float32),
        ],
    )
    return pl.pallas_call(
        flash_kernel,
        grid_spec=grid_spec,
        out_shape=jax.ShapeDtypeStruct(query_heads.shape, jnp.bfloat16),
        compiler_params=pltpu.CompilerParams(dimension_semantics=("arbitrary",)),
        interpret=INTERPRET,
    )(
        need,
        key_index,
        query_heads,
        kv_all,
        kv_all,
        seg_q.reshape(query_count, 1),
        pos_q.reshape(query_count, 1),
        seg_all.reshape(1, key_count),
        pos_all.reshape(1, key_count),
    )


def finish(state):
    running_max, running_sum, weighted_sum = state
    return (weighted_sum / running_sum[:, :, None]).astype(jnp.bfloat16)


def write_pages(kv_rows, page_table, width_dev):
    tok_count = kv_rows.shape[0]
    block_count = tok_count // PAGE
    devices = lax.axis_size("seq")
    capacity = (block_count + devices - 1) // devices
    owner = page_table // block_count
    owner_hot = (owner[:, None] == jnp.arange(devices, dtype=jnp.int32)[None, :]).astype(jnp.int32)
    earlier = jnp.cumsum(owner_hot, axis=0) - owner_hot
    occurrence = jnp.sum(earlier * owner_hot, axis=1)
    slot = owner * capacity + occurrence
    slot_hot = slot[None, :] == jnp.arange(devices * capacity, dtype=jnp.int32)[:, None]
    flat_blocks = kv_rows.reshape(block_count, PAGE * 2 * width_dev)
    outgoing = jnp.einsum(
        "sb,bx->sx", slot_hot.astype(jnp.bfloat16), flat_blocks, preferred_element_type=jnp.float32
    ).astype(jnp.bfloat16)
    labels = jnp.sum(jnp.where(slot_hot, (page_table % block_count)[None, :] + 1, 0), axis=1) - 1
    arrived, arrived_labels = (
        lax.all_to_all(outgoing, "seq", split_axis=0, concat_axis=0, tiled=True),
        lax.all_to_all(labels, "seq", split_axis=0, concat_axis=0, tiled=True),
    )
    place_hot = (
        arrived_labels[None, :] == jnp.arange(block_count, dtype=jnp.int32)[:, None]
    ).astype(jnp.bfloat16)
    placed = jnp.einsum("bs,sx->bx", place_hot, arrived, preferred_element_type=jnp.float32).astype(
        jnp.bfloat16
    )
    placed = placed.reshape(block_count, PAGE, 2 * width_dev)
    return (placed[:, :, :width_dev], placed[:, :, width_dev:])


def body(hidden, w_qkv, w_out, seg_ids, positions, page_table):
    tok_count = hidden.shape[0]
    full_rows = lax.all_gather(hidden, "tp", axis=1, tiled=True).astype(jnp.float32)
    row_mean = jnp.mean(full_rows, axis=1, keepdims=True)
    centred = full_rows - row_mean
    row_var = jnp.mean(centred * centred, axis=1, keepdims=True)
    normed = (centred * lax.rsqrt(row_var + EPSILON)).astype(jnp.bfloat16)
    projected = jnp.einsum("td,jde->jte", normed, w_qkv, preferred_element_type=jnp.float32)
    width_dev = w_qkv.shape[2]
    heads_dev = width_dev // HEAD_DIM
    cosine, sine_part = rope_tables(positions, HEAD_DIM)
    queries = rotate(
        projected[0].reshape(tok_count, heads_dev, HEAD_DIM), cosine, sine_part
    ).astype(jnp.bfloat16)
    key_heads = rotate(
        projected[1].reshape(tok_count, heads_dev, HEAD_DIM), cosine, sine_part
    ).astype(jnp.bfloat16)
    values = projected[2].astype(jnp.bfloat16)
    kv_rows = jnp.concatenate([key_heads.reshape(tok_count, width_dev), values], axis=1)
    query_heads = jnp.transpose(queries, (1, 0, 2))
    seq_count = lax.axis_size("seq")
    int_rows = jnp.concatenate([seg_ids, positions, page_table])
    int_all = lax.all_gather(int_rows, "seq", axis=0, tiled=False)
    seg_all = int_all[:, :tok_count].reshape(-1)
    pos_all = int_all[:, tok_count : 2 * tok_count].reshape(-1)
    table_all = int_all[:, 2 * tok_count :].reshape(-1)
    kv_all = lax.all_gather(kv_rows, "seq", axis=0, tiled=True)
    attended_heads = flash_attend(query_heads, seg_ids, positions, kv_all, seg_all, pos_all)
    block_count = tok_count // PAGE
    total_blocks = block_count * seq_count
    inverse = jnp.zeros((total_blocks,), jnp.int32).at[table_all].set(
        jnp.arange(total_blocks, dtype=jnp.int32)
    )
    mine = lax.dynamic_slice(inverse, (lax.axis_index("seq") * block_count,), (block_count,))
    placed = jnp.take(kv_all.reshape(total_blocks, PAGE, 2 * width_dev), mine, axis=0)
    k_cache = placed[:, :, :width_dev]
    v_cache = placed[:, :, width_dev:]
    attended = jnp.transpose(attended_heads, (1, 0, 2)).reshape(tok_count, width_dev)
    partial_out = jnp.dot(attended, w_out, preferred_element_type=jnp.float32).astype(jnp.bfloat16)
    delta = lax.psum_scatter(partial_out, "tp", scatter_dimension=1, tiled=True)
    return (delta, k_cache, v_cache)


def solution(mesh):
    in_specs = (P("seq", "tp"), P(None, None, "tp"), P("tp", None), P("seq"), P("seq"), P("seq"))
    out_specs = (P("seq", "tp"), P("seq", None, "tp"), P("seq", None, "tp"))
    return jax.shard_map(body, mesh=mesh, in_specs=in_specs, out_specs=out_specs, check_vma=False)
```
